32 devices in a mesh: seq: 8 (over z, x), chan: 4 (over y, core).
Axes of the slice: x: 2, y: 2, z: 4, core: 2. Of those that a mesh axis runs over, the one named last changes fastest.
Arguments:
- query_gate: bfloat16 [4096, 8192], P('seq', 'chan'), may hold values from -23 to 23
- key_gate: bfloat16 [4096, 8192], P('seq', 'chan'), may hold values from -6 to 6
- value_input: bfloat16 [4096, 8192], P('seq', 'chan'), may hold values from -6 to 6
- filter_taps: bfloat16 [4096, 128], P('seq', 'chan'), may hold values from -1 to 1
- norm_gain: float32 [8192], P('chan'), may hold values from 0.5 to 1.5
Outputs:
- gated: bfloat16 [4096, 8192], P('seq', 'chan')
- normed: bfloat16 [4096, 8192], P('seq', 'chan')
The draws below stay inside these ranges and needn't reach their ends.
All inputs are finite; a program needn't handle non-finite values.
Results may differ from the reference program's by a relative error of at most 0.01.
Values may be sent and summed in bfloat16 or wider, within the bound.
No kernel may reach another device: no remote copies, remote signals or barrier semaphores. Data moves between devices by JAX's collectives and lax.ppermute only.
A program may use at most 64 MiB of HBM per device.

```python
import math
import jax
import jax.numpy as jnp
from jax import lax

D = 8192
GROUPS = 128
TOK_DEV = 512
LENGTH = 4096
N_SEQ = 8


def draw_query_gate(key, part):
    base_key = jax.random.fold_in(key, 11)
    subkeys = jax.random.split(base_key, 3)
    channel_pos = jnp.arange(D, dtype=jnp.float32) / D
    channel_rough = jax.random.uniform(subkeys[1], (D,), dtype=jnp.float32)
    channel_scale = 10.0 ** (0.5 * channel_pos + 0.5 * channel_rough - 0.5)
    token_scale = 10.0 ** (0.5 * jax.random.uniform(subkeys[2], (LENGTH, 1), dtype=jnp.float32) - 0.25)
    values = jax.random.truncated_normal(subkeys[0], -4.0, 4.0, (LENGTH, D), dtype=jnp.float32)
    return (values * channel_scale[None, :] * token_scale).astype(jnp.bfloat16)


def draw_filter_taps(key, part):
    base_key = jax.random.fold_in(key, 23)
    subkeys = jax.random.split(base_key, 2)
    upper_log = math.log(4.0 * LENGTH)
    lower_log = math.log(32.0)
    decay_length = jnp.exp(jax.random.uniform(subkeys[1], (GROUPS,), dtype=jnp.float32, minval=lower_log, maxval=upper_log))
    positions = jnp.arange(LENGTH, dtype=jnp.float32)[:, None]
    envelope = jnp.exp(-positions / decay_length[None, :]) * jnp.sqrt(2.0 / decay_length)[None, :]
    noise = jax.random.truncated_normal(subkeys[0], -4.0, 4.0, (LENGTH, GROUPS), dtype=jnp.float32)
    return (noise * envelope).astype(jnp.bfloat16)


def block_scale(own_key, extent, cuts, smallest, top_value):
    factor_of, own = 1.0, jax.random.fold_in(own_key, 6)
    for dim, shards_of in cuts:
        steps = jnp.exp(jax.random.uniform(jax.random.fold_in(own, dim), (shards_of,), jnp.float32, smallest / len(cuts), top_value / len(cuts)))
        factor_of = factor_of * jnp.repeat(steps, extent[dim] // shards_of).reshape([-1 if axis == dim else 1 for axis in range(len(extent))])
    return factor_of


def gaussian(stream_key, dims, scale, most, cuts=(), kind=jnp.bfloat16):
    gain = block_scale(stream_key, dims, cuts, -0.22, 0.18) if cuts else 1.0
    drawn = jax.random.normal(stream_key, dims, jnp.float32) * scale * gain
    return jnp.minimum(jnp.maximum(drawn, -most), most).astype(kind)


def setup_inputs(seed: int = 0) -> dict:
    keys = jax.random.split(jax.random.key(seed), 6)
    query_gate = draw_query_gate(jax.random.fold_in(keys[5], 71), 0)
    key_gate = gaussian(keys[1], (LENGTH, D), 1.0, 6.0, ((0, 8), (1, 4)))
    value_input = gaussian(keys[2], (LENGTH, D), 1.0, 6.0, ((0, 8), (1, 4)))
    filter_taps = draw_filter_taps(jax.random.fold_in(keys[5], 71), 0)
    norm_gain = jnp.clip(1.0 + 0.1 * jax.random.normal(keys[4], (D,), jnp.float32), 0.5, 1.5)
    return {"query_gate": query_gate, "key_gate": key_gate, "value_input": value_input, "filter_taps": filter_taps, "norm_gain": norm_gain}


norm_eps = 1e-05

def angle_table(rows_count, cols_count, row_start, col_start, period):
    row_ids = row_start + lax.iota(jnp.int32, rows_count)
    col_ids = col_start + lax.iota(jnp.int32, cols_count)
    phases = row_ids[:, None] * col_ids[None, :] % period
    return phases.astype(jnp.float32) * (2.0 * math.pi / period)

def block_matrix(rows_count, cols_count, period):
    phases = angle_table(rows_count, cols_count, 0, 0, period)
    return jnp.stack([jnp.cos(phases), -jnp.sin(phases)]).astype(jnp.bfloat16)

def line_matrix(length, direction):
    phases = angle_table(length, length, 0, 0, length)
    cosine = jnp.cos(phases)
    sine_part = jnp.sin(phases) * direction
    upper = jnp.concatenate([cosine, sine_part], axis=1)
    lower = jnp.concatenate([-sine_part, cosine], axis=1)
    return jnp.concatenate([upper, lower], axis=0).astype(jnp.bfloat16)

def twiddle(halves, row_start, col_start, period, direction):
    phases = angle_table(halves.shape[1], halves.shape[2], row_start, col_start, period)
    cosine = jnp.cos(phases)[:, :, None]
    sine_part = direction * jnp.sin(phases)[:, :, None]
    real_part = halves[0] * cosine - halves[1] * sine_part
    imaginary = halves[1] * cosine + halves[0] * sine_part
    return jnp.stack([real_part, imaginary])

def blocks_forward(blocks_in, matrix):
    return jnp.einsum('abc,rak->rbkc', blocks_in.astype(jnp.float32), matrix.astype(jnp.float32))

def line_apply(halves, matrix):
    dims_all = halves.shape
    flattened = halves.reshape(2 * dims_all[1], dims_all[2] * dims_all[3])
    return jnp.dot(matrix, flattened, preferred_element_type=jnp.float32).reshape(dims_all)

def apply_filter(spectrum, filter_spec):
    dims_all = spectrum.shape
    group_count = filter_spec.shape[3]
    grouped = spectrum.reshape(dims_all[0], dims_all[1], dims_all[2], group_count, dims_all[3] // group_count)
    filter_real = filter_spec[0][..., None]
    filter_imaginary = filter_spec[1][..., None]
    real_part = grouped[0] * filter_real - grouped[1] * filter_imaginary
    imaginary = grouped[0] * filter_imaginary + grouped[1] * filter_real
    return jnp.stack([real_part, imaginary]).reshape(dims_all).astype(jnp.bfloat16)

def blocks_inverse(halves, matrix, factor):
    summed = jnp.einsum('rbkc,rka->abc', halves.astype(jnp.float32), matrix.astype(jnp.float32))
    return (summed * factor).astype(jnp.bfloat16)

def reference(query_gate, key_gate, value_input, filter_taps, norm_gain):
    blocks = N_SEQ
    tokens = TOK_DEV
    periods = 2 * LENGTH
    group_width = D // GROUPS
    product = (key_gate.astype(jnp.float32) * value_input.astype(jnp.float32)).astype(jnp.bfloat16)
    first_matrix = block_matrix(blocks, 2 * blocks, 2 * blocks)
    last_matrix = block_matrix(2 * blocks, blocks, 2 * blocks)
    line_forward = line_matrix(tokens, 1.0)
    line_backward = line_matrix(tokens, -1.0)

    def convolve(group):
        start = (group * group_width).astype(jnp.int32)
        data_rows = lax.dynamic_slice_in_dim(product, start, group_width, 1).reshape(blocks, tokens, group_width)
        taps_rows = lax.dynamic_slice_in_dim(filter_taps, group.astype(jnp.int32), 1, 1).reshape(blocks, tokens, 1)
        data_spread = twiddle(blocks_forward(data_rows, first_matrix), 0, 0, periods, -1.0).astype(jnp.bfloat16)
        taps_spread = twiddle(blocks_forward(taps_rows, first_matrix), 0, 0, periods, -1.0).astype(jnp.bfloat16)
        spectrum = line_apply(data_spread, line_forward)
        taps_spectrum = line_apply(taps_spread, line_forward)
        filtered = apply_filter(spectrum, taps_spectrum)
        returned = twiddle(line_apply(filtered, line_backward), 0, 0, periods, 1.0).astype(jnp.bfloat16)
        local_blocks = blocks_inverse(returned, last_matrix, 1.0 / periods)
        return local_blocks.reshape(LENGTH, group_width)
    pieces = lax.map(convolve, jnp.arange(GROUPS, dtype=jnp.int32))
    convolved = jnp.transpose(pieces, (1, 0, 2)).reshape(LENGTH, D)
    gated_full = query_gate.astype(jnp.float32) * convolved.astype(jnp.float32)
    mean_square = lax.optimization_barrier(jnp.mean(gated_full * gated_full, axis=1, keepdims=True))
    normed = gated_full * lax.rsqrt(mean_square + norm_eps) * norm_gain.astype(jnp.float32)[None, :]
    return (gated_full.astype(jnp.bfloat16), normed.astype(jnp.bfloat16))
```

```python
import functools
import math

import jax
import jax.numpy as jnp
from jax import lax
from jax.experimental import pallas as pl
from jax.experimental.pallas import tpu as pltpu
from jax.sharding import PartitionSpec as P


D = 8192
GROUPS = 128


norm_eps = 1e-05


def angle_table(rows_count, cols_count, period):
    row_ids = lax.iota(jnp.int32, rows_count)
    col_ids = lax.iota(jnp.int32, cols_count)
    phases = row_ids[:, None] * col_ids[None, :] % period
    return phases.astype(jnp.float32) * (2.0 * math.pi / period)


def block_matrix(rows_count, cols_count, period):
    phases = angle_table(rows_count, cols_count, period)
    return jnp.stack([jnp.cos(phases), -jnp.sin(phases)]).astype(jnp.bfloat16)


def line_matrix(length, direction):
    phases = angle_table(length, length, length)
    cosine = jnp.cos(phases)
    sine_part = jnp.sin(phases) * direction
    upper = jnp.concatenate([cosine, sine_part], axis=1)
    lower = jnp.concatenate([-sine_part, cosine], axis=1)
    return jnp.concatenate([upper, lower], axis=0).astype(jnp.bfloat16)


def twiddle_minor(real_in, imag_in, period, direction):
    phases = angle_table(real_in.shape[1], real_in.shape[2], period)
    cosine = jnp.cos(phases)[None, :, :]
    sine_part = direction * jnp.sin(phases)[None, :, :]
    real_part = real_in * cosine - imag_in * sine_part
    imaginary = imag_in * cosine + real_in * sine_part
    return (real_part, imaginary)


def spectrum_minor(rows_in, first_matrix, right_forward, periods):
    spread = jnp.einsum("cab,rak->rckb", rows_in, first_matrix, preferred_element_type=jnp.float32)
    real_part, imaginary = twiddle_minor(spread[0], spread[1], periods, -1.0)
    joined = jnp.concatenate(
        [real_part.astype(jnp.bfloat16), imaginary.astype(jnp.bfloat16)], axis=2
    )
    return jnp.einsum("ckb,bm->ckm", joined, right_forward, preferred_element_type=jnp.float32)


def dense_body(query_gate, key_gate, value_input, filter_taps, norm_gain):
    tokens, channels = key_gate.shape
    blocks = lax.axis_size("seq")
    periods = 2 * tokens * blocks
    product = (key_gate.astype(jnp.float32) * value_input.astype(jnp.float32)).astype(jnp.bfloat16)
    first_matrix = block_matrix(blocks, 2 * blocks, 2 * blocks)
    last_matrix = block_matrix(2 * blocks, blocks, 2 * blocks)
    line_forward = line_matrix(tokens, 1.0)
    line_backward = line_matrix(tokens, -1.0)
    width_here = channels // blocks
    group_width = D // GROUPS
    repeat_count = max(1, group_width // width_here)
    taps_wide = jnp.repeat(filter_taps, repeat_count, axis=1)
    data_major = jnp.transpose(product)
    taps_major = jnp.transpose(taps_wide)
    data_whole, taps_whole = (
        lax.all_to_all(data_major, "seq", split_axis=0, concat_axis=1, tiled=True),
        lax.all_to_all(taps_major, "seq", split_axis=0, concat_axis=1, tiled=True),
    )
    taps_cols = taps_whole.shape[0]
    data_rows = data_whole.reshape(width_here, blocks, tokens)
    taps_rows = taps_whole.reshape(taps_cols, blocks, tokens)
    right_forward = jnp.transpose(line_forward)
    right_backward = jnp.transpose(line_backward)
    spectrum = spectrum_minor(data_rows, first_matrix, right_forward, periods)
    taps_spectrum = spectrum_minor(taps_rows, first_matrix, right_forward, periods)
    grouped = spectrum.reshape(taps_cols, width_here // taps_cols, 2 * blocks, 2 * tokens)
    spec_real = grouped[..., :tokens]
    spec_imag = grouped[..., tokens:]
    filter_real = taps_spectrum[:, None, :, :tokens]
    filter_imag = taps_spectrum[:, None, :, tokens:]
    filtered_real = (spec_real * filter_real - spec_imag * filter_imag).astype(jnp.bfloat16)
    filtered_imag = (spec_real * filter_imag + spec_imag * filter_real).astype(jnp.bfloat16)
    filtered = jnp.concatenate([filtered_real, filtered_imag], axis=3).reshape(
        width_here, 2 * blocks, 2 * tokens
    )
    inverted = jnp.einsum(
        "ckm,mb->ckb", filtered, right_backward, preferred_element_type=jnp.float32
    )
    back_real, back_imag = twiddle_minor(
        inverted[..., :tokens], inverted[..., tokens:], periods, 1.0
    )
    returned = jnp.stack([back_real, back_imag]).astype(jnp.bfloat16)
    summed = jnp.einsum("rckb,rka->cab", returned, last_matrix, preferred_element_type=jnp.float32)
    local_blocks = (
        (summed * (1.0 / periods)).astype(jnp.bfloat16).reshape(width_here, blocks * tokens)
    )
    convolved_major = lax.all_to_all(local_blocks, "seq", split_axis=1, concat_axis=0, tiled=True)
    convolved = jnp.transpose(convolved_major)
    gated_full = query_gate.astype(jnp.float32) * convolved.astype(jnp.float32)
    partial_squares = jnp.sum(gated_full * gated_full, axis=1)
    square_sum = lax.psum(partial_squares, "chan")
    inverse_rms = lax.rsqrt(square_sum / D + norm_eps)
    normed = gated_full * inverse_rms[:, None] * norm_gain[None, :]
    return (gated_full.astype(jnp.bfloat16), normed.astype(jnp.bfloat16))


LANES = 128
HALF = 256


def pairs_of(blocks, delta):
    return [(source, source ^ delta) for source in range(blocks)]


def product_kernel(blocks, tokens, with_taps, seq_ref, *refs):
    keys, values = refs[:blocks], refs[blocks : 2 * blocks]
    taps_ref, outs = refs[2 * blocks], refs[2 * blocks + 1 :]
    for delta in range(blocks):
        wide = keys[delta][...].astype(jnp.float32) * values[delta][...].astype(jnp.float32)
        outs[delta][pl.ds(0, tokens), :] = wide.astype(jnp.bfloat16)
        if with_taps:
            rows = taps_ref.shape[1]
            outs[delta][pl.ds(tokens, rows), :] = taps_ref[seq_ref[0] ^ delta]


def make_product(seq_index, key_gate, value_input, taps, blocks, chunk, chunks, with_taps):
    tokens = key_gate.shape[0]
    rows = tokens + (taps.shape[1] if with_taps else 0)
    column = [
        pl.BlockSpec((tokens, LANES), functools.partial(column_map, delta, chunk, chunks))
        for delta in range(blocks)
    ]
    taps_spec = pl.BlockSpec(taps.shape, lambda step, seq_ref: (0, 0, 0))
    return pl.pallas_call(
        functools.partial(product_kernel, blocks, tokens, with_taps),
        out_shape=[jax.ShapeDtypeStruct((rows, LANES), jnp.bfloat16)] * blocks,
        grid_spec=pltpu.PrefetchScalarGridSpec(
            num_scalar_prefetch=1,
            grid=(1,),
            in_specs=column + column + [taps_spec],
            out_specs=[pl.BlockSpec((rows, LANES), lambda step, seq_ref: (0, 0))] * blocks,
        ),
        cost_estimate=pl.CostEstimate(
            flops=tokens * LANES * blocks, bytes_accessed=6 * tokens * LANES * blocks, transcendentals=0
        ),
        name=f"product_{chunk}",
    )(seq_index, *[key_gate] * blocks, *[value_input] * blocks, taps)


def column_map(delta, chunk, chunks, step, seq_ref):
    return (0, (seq_ref[0] ^ delta) * chunks + chunk)


def toeplitz_kernel(blocks, groups, per_chunk, seq_ref, *refs):
    taps, outs, lines = refs[:blocks], refs[blocks:-1], refs[-1]
    lines[...] = jnp.zeros_like(lines)
    for delta in range(blocks):
        source = seq_ref[0] ^ delta
        rows = taps[delta][...].astype(jnp.float32)
        for group in range(groups):
            lines[group, source + 1, pl.ds(0, 4), :] = rows[4 * group : 4 * group + 4]

    def one_line(group, block, index):
        at = index % 4
        return lines[group, block + 1 + (index - at) // 4, pl.ds(at, 1), :]

    def fill(block, carry):
        for group in range(groups):
            out, top = outs[group // per_chunk], (group % per_chunk) * HALF
            for index in range(-1, 4):
                base = jnp.concatenate(
                    [one_line(group, block, index), one_line(group, block, index - 1)], axis=1
                )
                wide = jnp.broadcast_to(base, (LANES, 2 * LANES))
                turned = pltpu.roll(wide, 1, 1, stride=1, stride_axis=0)
                square = turned[:, LANES:].astype(jnp.bfloat16)
                for row, col, want in (
                    (0, 0, 0), (1, 0, 1), (0, 1, -1), (1, 1, 0),
                    (0, 2, 2), (1, 2, 3), (0, 3, 1), (1, 3, 2),
                ):
                    if want == index:
                        out[block, pl.ds(top + row * LANES, LANES), pl.ds(col * LANES, LANES)] = square
        return carry

    lax.fori_loop(0, blocks, fill, 0)


def make_toeplitz(seq_index, received, blocks, tokens, groups, chunks):
    per_chunk = groups // chunks
    tap_rows = received[0].shape[0] - tokens
    shape = (blocks, per_chunk * HALF, 2 * HALF)
    return pl.pallas_call(
        functools.partial(toeplitz_kernel, blocks, groups, per_chunk),
        out_shape=[jax.ShapeDtypeStruct(shape, jnp.bfloat16)] * chunks,
        grid_spec=pltpu.PrefetchScalarGridSpec(
            num_scalar_prefetch=1,
            grid=(1,),
            in_specs=[
                pl.BlockSpec((tap_rows, LANES), lambda step, seq_ref: (tokens // tap_rows, 0))
            ] * blocks,
            out_specs=[pl.BlockSpec(shape, lambda step, seq_ref: (0, 0, 0))] * chunks,
            scratch_shapes=[pltpu.VMEM((groups, blocks + 1, 8, LANES), jnp.float32)],
        ),
        cost_estimate=pl.CostEstimate(
            flops=0, bytes_accessed=4 * chunks * blocks * per_chunk * HALF * HALF, transcendentals=0
        ),
        name="toeplitz",
    )(seq_index, *received)


def conv_kernel(blocks, per_chunk, seq_ref, *refs):
    pieces, table, outs = refs[:blocks], refs[blocks], refs[blocks + 1 : -2]
    past, total = refs[-2], refs[-1]
    last = 2 * blocks - 1
    past[pl.ds(2 * blocks * HALF, HALF), :] = jnp.zeros((HALF, LANES), jnp.bfloat16)
    for delta in range(blocks):
        source = seq_ref[0] ^ delta
        for part in range(2):
            place = pl.multiple_of((last - part - 2 * source) * HALF, HALF)
            past[pl.ds(place, HALF), :] = pieces[delta][pl.ds(part * HALF, HALF), :]
    lane = lax.broadcasted_iota(jnp.int32, (HALF, LANES), 1) * per_chunk // LANES
    for delta in range(blocks):
        target = seq_ref[0] ^ delta

        def term(lag):
            place = pl.multiple_of((last - 2 * target + 2 * lag) * HALF, HALF)
            left = past[pl.ds(place, 2 * HALF), :]
            right = past[pl.ds(pl.multiple_of(place - HALF, HALF), 2 * HALF), :]
            return jnp.dot(
                table[lag],
                jnp.concatenate([left, right], axis=1),
                preferred_element_type=jnp.float32,
            )

        total[...] = term(0)

        def step(lag, carry):
            total[...] += term(lag)
            return carry

        lax.fori_loop(1, target + 1, step, 0)
        for part in range(2):
            columns = pl.ds(part * LANES, LANES)
            chosen = total[pl.ds(0, HALF), columns]
            for group in range(1, per_chunk):
                chosen = jnp.where(lane == group, total[pl.ds(group * HALF, HALF), columns], chosen)
            outs[delta][pl.ds(part * HALF, HALF), :] = chosen.astype(jnp.bfloat16)


def make_conv(seq_index, pieces, table, blocks, tokens, chunk):
    per_chunk = table.shape[1] // HALF
    flops = 4 * HALF * HALF * HALF * per_chunk * blocks * (blocks + 1)
    return pl.pallas_call(
        functools.partial(conv_kernel, blocks, per_chunk),
        out_shape=[jax.ShapeDtypeStruct((tokens, LANES), jnp.bfloat16)] * blocks,
        grid_spec=pltpu.PrefetchScalarGridSpec(
            num_scalar_prefetch=1,
            grid=(1,),
            in_specs=[pl.BlockSpec((tokens, LANES), lambda step, seq_ref: (0, 0))] * blocks
            + [pl.BlockSpec(table.shape, lambda step, seq_ref: (0, 0, 0))],
            out_specs=[pl.BlockSpec((tokens, LANES), lambda step, seq_ref: (0, 0))] * blocks,
            scratch_shapes=[
                pltpu.VMEM(((2 * blocks + 1) * HALF, LANES), jnp.bfloat16),
                pltpu.VMEM((per_chunk * HALF, HALF), jnp.float32),
            ],
        ),
        cost_estimate=pl.CostEstimate(
            flops=flops, bytes_accessed=2 * table.size + 4 * blocks * tokens * LANES, transcendentals=0
        ),
        name=f"convolve_{chunk}",
    )(seq_index, *pieces, table)


def squares_kernel(blocks, seq_ref, *refs):
    gates, pieces, out = refs[:blocks], refs[blocks : 2 * blocks], refs[-1]
    total = None
    for delta in range(blocks):
        gated = gates[delta][...].astype(jnp.float32) * pieces[delta][...].astype(jnp.float32)
        total = gated * gated if total is None else total + gated * gated
    out[...] = jnp.sum(jnp.transpose(total), axis=0, keepdims=True)


def make_squares(seq_index, query_gate, pieces, blocks, chunk, chunks):
    tokens = query_gate.shape[0]
    return pl.pallas_call(
        functools.partial(squares_kernel, blocks),
        out_shape=jax.ShapeDtypeStruct((1, tokens), jnp.float32),
        grid_spec=pltpu.PrefetchScalarGridSpec(
            num_scalar_prefetch=1,
            grid=(1,),
            in_specs=[
                pl.BlockSpec((tokens, LANES), functools.partial(column_map, delta, chunk, chunks))
                for delta in range(blocks)
            ]
            + [pl.BlockSpec((tokens, LANES), lambda step, seq_ref: (0, 0))] * blocks,
            out_specs=pl.BlockSpec((1, tokens), lambda step, seq_ref: (0, 0)),
        ),
        cost_estimate=pl.CostEstimate(
            flops=3 * tokens * LANES * blocks, bytes_accessed=4 * tokens * LANES * blocks, transcendentals=0
        ),
        name=f"squares_{chunk}",
    )(seq_index, *[query_gate] * blocks, *pieces)


def finish_kernel(blocks, chunks, seq_ref, gate_ref, gain_ref, sum_ref, *refs):
    pieces, gated_ref, normed_ref = refs[:-2], refs[-2], refs[-1]
    rows = gate_ref.shape[0]
    inverse = lax.rsqrt(sum_ref[...] / D + norm_eps)
    scale = jnp.transpose(jnp.broadcast_to(inverse, (LANES, rows)))
    for delta in range(blocks):
        for chunk in range(chunks):
            place = pl.multiple_of(((seq_ref[0] ^ delta) * chunks + chunk) * LANES, LANES)
            columns = pl.ds(place, LANES)
            piece = pieces[chunk * blocks + delta][...].astype(jnp.float32)
            gated = gate_ref[:, columns].astype(jnp.float32) * piece
            gated_ref[:, columns] = gated.astype(jnp.bfloat16)
            normed_ref[:, columns] = (gated * scale * gain_ref[:, columns]).astype(jnp.bfloat16)


def make_finish(seq_index, query_gate, norm_gain, square_sum, pieces, blocks, chunks):
    tokens, channels = query_gate.shape
    rows = LANES
    row_spec = pl.BlockSpec((rows, channels), lambda step, seq_ref: (step, 0))
    return pl.pallas_call(
        functools.partial(finish_kernel, blocks, chunks),
        out_shape=[jax.ShapeDtypeStruct((tokens, channels), jnp.bfloat16)] * 2,
        grid_spec=pltpu.PrefetchScalarGridSpec(
            num_scalar_prefetch=1,
            grid=(tokens // rows,),
            in_specs=[
                row_spec,
                pl.BlockSpec((1, channels), lambda step, seq_ref: (0, 0)),
                pl.BlockSpec((1, rows), lambda step, seq_ref: (0, step)),
            ]
            + [pl.BlockSpec((rows, LANES), lambda step, seq_ref: (step, 0))] * (blocks * chunks),
            out_specs=[row_spec, row_spec],
        ),
        cost_estimate=pl.CostEstimate(
            flops=4 * tokens * channels, bytes_accessed=8 * tokens * channels, transcendentals=tokens
        ),
        name="finish",
    )(seq_index, query_gate, norm_gain[None, :], square_sum, *pieces)


def exchange(pieces, blocks):
    order = sorted(range(1, blocks), reverse=True)
    moved = {delta: lax.ppermute(pieces[delta], "seq", pairs_of(blocks, delta)) for delta in order}
    return [pieces[0]] + [moved[delta] for delta in range(1, blocks)]


def tiles_fit(tokens, channels, groups, blocks):
    if blocks & (blocks - 1) or tokens != 2 * HALF or channels % (blocks * LANES):
        return False
    width_here, group_width = channels // blocks, channels // groups
    return LANES % group_width == 0 and width_here % group_width == 0


def body(query_gate, key_gate, value_input, filter_taps, norm_gain):
    tokens, channels = key_gate.shape
    blocks = lax.axis_size("seq")
    groups_here = filter_taps.shape[1]
    if not tiles_fit(tokens, channels, groups_here, blocks):
        return dense_body(query_gate, key_gate, value_input, filter_taps, norm_gain)
    chunks = channels // (blocks * LANES)
    groups = groups_here // blocks
    seq_index = lax.axis_index("seq").astype(jnp.int32)[None]
    taps = jnp.transpose(filter_taps).reshape(blocks, groups * tokens // LANES, LANES)[:, :, ::-1]

    received = []
    for chunk in range(chunks):
        sent = make_product(
            seq_index, key_gate, value_input, taps, blocks, chunk, chunks, chunk == 0
        )
        received.append(exchange(sent, blocks))
    tables = make_toeplitz(seq_index, received[0], blocks, tokens, groups, chunks)
    returned = []
    square_sum = 0.0
    for chunk in range(chunks):
        local = make_conv(seq_index, received[chunk], tables[chunk], blocks, tokens, chunk)
        returned.append(exchange(local, blocks))
        square_sum += make_squares(seq_index, query_gate, returned[chunk], blocks, chunk, chunks)
    square_sum = lax.psum(square_sum, "chan")
    pieces = [piece for chunk in returned for piece in chunk]
    gated, normed = make_finish(
        seq_index, query_gate, norm_gain, square_sum, pieces, blocks, chunks
    )
    return (gated, normed)


def solution(mesh):
    placed = (P("seq", "chan"), P("seq", "chan"), P("seq", "chan"), P("seq", "chan"), P("chan"))
    return jax.shard_map(
        body,
        mesh=mesh,
        in_specs=placed,
        out_specs=(P("seq", "chan"), P("seq", "chan")),
        check_vma=False,
    )
```

```python
import functools
import math

import jax
import jax.numpy as jnp
from jax import lax
from jax.experimental import pallas as pl
from jax.experimental.pallas import tpu as pltpu
from jax.sharding import PartitionSpec as P


D = 8192
GROUPS = 128


norm_eps = 1e-05


def angle_table(rows_count, cols_count, period):
    row_ids = lax.iota(jnp.int32, rows_count)
    col_ids = lax.iota(jnp.int32, cols_count)
    phases = row_ids[:, None] * col_ids[None, :] % period
    return phases.astype(jnp.float32) * (2.0 * math.pi / period)


def block_matrix(rows_count, cols_count, period):
    phases = angle_table(rows_count, cols_count, period)
    return jnp.stack([jnp.cos(phases), -jnp.sin(phases)]).astype(jnp.bfloat16)


def line_matrix(length, direction):
    phases = angle_table(length, length, length)
    cosine = jnp.cos(phases)
    sine_part = jnp.sin(phases) * direction
    upper = jnp.concatenate([cosine, sine_part], axis=1)
    lower = jnp.concatenate([-sine_part, cosine], axis=1)
    return jnp.concatenate([upper, lower], axis=0).astype(jnp.bfloat16)


def twiddle_minor(real_in, imag_in, period, direction):
    phases = angle_table(real_in.shape[1], real_in.shape[2], period)
    cosine = jnp.cos(phases)[None, :, :]
    sine_part = direction * jnp.sin(phases)[None, :, :]
    real_part = real_in * cosine - imag_in * sine_part
    imaginary = imag_in * cosine + real_in * sine_part
    return (real_part, imaginary)


def spectrum_minor(rows_in, first_matrix, right_forward, periods):
    spread = jnp.einsum("cab,rak->rckb", rows_in, first_matrix, preferred_element_type=jnp.float32)
    real_part, imaginary = twiddle_minor(spread[0], spread[1], periods, -1.0)
    joined = jnp.concatenate(
        [real_part.astype(jnp.bfloat16), imaginary.astype(jnp.bfloat16)], axis=2
    )
    return jnp.einsum("ckb,bm->ckm", joined, right_forward, preferred_element_type=jnp.float32)


def dense_body(query_gate, key_gate, value_input, filter_taps, norm_gain):
    tokens, channels = key_gate.shape
    blocks = lax.axis_size("seq")
    periods = 2 * tokens * blocks
    product = (key_gate.astype(jnp.float32) * value_input.astype(jnp.float32)).astype(jnp.bfloat16)
    first_matrix = block_matrix(blocks, 2 * blocks, 2 * blocks)
    last_matrix = block_matrix(2 * blocks, blocks, 2 * blocks)
    line_forward = line_matrix(tokens, 1.0)
    line_backward = line_matrix(tokens, -1.0)
    width_here = channels // blocks
    group_width = D // GROUPS
    repeat_count = max(1, group_width // width_here)
    taps_wide = jnp.repeat(filter_taps, repeat_count, axis=1)
    data_major = jnp.transpose(product)
    taps_major = jnp.transpose(taps_wide)
    data_whole, taps_whole = (
        lax.all_to_all(data_major, "seq", split_axis=0, concat_axis=1, tiled=True),
        lax.all_to_all(taps_major, "seq", split_axis=0, concat_axis=1, tiled=True),
    )
    taps_cols = taps_whole.shape[0]
    data_rows = data_whole.reshape(width_here, blocks, tokens)
    taps_rows = taps_whole.reshape(taps_cols, blocks, tokens)
    right_forward = jnp.transpose(line_forward)
    right_backward = jnp.transpose(line_backward)
    spectrum = spectrum_minor(data_rows, first_matrix, right_forward, periods)
    taps_spectrum = spectrum_minor(taps_rows, first_matrix, right_forward, periods)
    grouped = spectrum.reshape(taps_cols, width_here // taps_cols, 2 * blocks, 2 * tokens)
    spec_real = grouped[..., :tokens]
    spec_imag = grouped[..., tokens:]
    filter_real = taps_spectrum[:, None, :, :tokens]
    filter_imag = taps_spectrum[:, None, :, tokens:]
    filtered_real = (spec_real * filter_real - spec_imag * filter_imag).astype(jnp.bfloat16)
    filtered_imag = (spec_real * filter_imag + spec_imag * filter_real).astype(jnp.bfloat16)
    filtered = jnp.concatenate([filtered_real, filtered_imag], axis=3).reshape(
        width_here, 2 * blocks, 2 * tokens
    )
    inverted = jnp.einsum(
        "ckm,mb->ckb", filtered, right_backward, preferred_element_type=jnp.float32
    )
    back_real, back_imag = twiddle_minor(
        inverted[..., :tokens], inverted[..., tokens:], periods, 1.0
    )
    returned = jnp.stack([back_real, back_imag]).astype(jnp.bfloat16)
    summed = jnp.einsum("rckb,rka->cab", returned, last_matrix, preferred_element_type=jnp.float32)
    local_blocks = (
        (summed * (1.0 / periods)).astype(jnp.bfloat16).reshape(width_here, blocks * tokens)
    )
    convolved_major = lax.all_to_all(local_blocks, "seq", split_axis=1, concat_axis=0, tiled=True)
    convolved = jnp.transpose(convolved_major)
    gated_full = query_gate.astype(jnp.float32) * convolved.astype(jnp.float32)
    partial_squares = jnp.sum(gated_full * gated_full, axis=1)
    square_sum = lax.psum(partial_squares, "chan")
    inverse_rms = lax.rsqrt(square_sum / D + norm_eps)
    normed = gated_full * inverse_rms[:, None] * norm_gain[None, :]
    return (gated_full.astype(jnp.bfloat16), normed.astype(jnp.bfloat16))


LANES = 128
HALF = 256
VMEM_BYTES = 20 << 20
SMALL_BYTES = 10 << 20
FIRST_BYTES = 62 << 20
PRODUCT_BYTES = 58 << 20
ANYWHERE = pl.BlockSpec(memory_space=pl.ANY)
ORDERS = (
    (6, 7, 4, 5, 2, 3, 1),
    (1, 2, 3, 4, 5, 6, 7),
    (1, 2, 3, 4, 5, 6, 7),
    (1, 2, 3, 4, 5, 6, 7),
)
FINISH_ROWS = 256


def pairs_of(blocks, delta):
    return [(source, source ^ delta) for source in range(blocks)]


def tap_rows_of(taps_ref, rows_ref, blocks):
    groups, count = taps_ref.shape[0] // blocks, taps_ref.shape[1] // LANES
    mirror = lax.broadcasted_iota(jnp.int32, (LANES, LANES), 0) + lax.broadcasted_iota(
        jnp.int32, (LANES, LANES), 1
    )
    mirror = (mirror == LANES - 1).astype(jnp.float32).astype(jnp.bfloat16)
    for part in range(count):
        line = taps_ref[:, pl.ds(part * LANES, LANES)]
        line = jnp.dot(line, mirror, preferred_element_type=jnp.float32)
        for block in range(blocks):
            rows_ref[block, pl.ds(part * groups, groups), :] = line[block * groups : (block + 1) * groups]


def product_kernel(blocks, deltas, tokens, with_taps, seq_ref, *refs):
    count = len(deltas)
    keys, values = refs[:count], refs[count : 2 * count]
    outs = refs[-count - 1 : -1] if with_taps else refs[-count:]
    if with_taps:
        taps_ref, rows_ref = refs[2 * count], refs[-1]
        tap_rows_of(taps_ref, rows_ref, blocks)
    for index, delta in enumerate(deltas):
        wide = keys[index][...].astype(jnp.float32) * values[index][...].astype(jnp.float32)
        outs[index][pl.ds(0, tokens), :] = wide.astype(jnp.bfloat16)
        if with_taps:
            lines = rows_ref[seq_ref[0] ^ delta]
            outs[index][pl.ds(tokens, lines.shape[0]), :] = lines.astype(jnp.bfloat16)


def make_product(seq_index, key_gate, value_input, taps, blocks, deltas, chunk, chunks, vmem_bytes):
    tokens, count = key_gate.shape[0], len(deltas)
    with_taps = taps is not None
    tap_rows = taps.size // (blocks * LANES) if with_taps else 0
    rows = tokens + tap_rows
    column = [
        pl.BlockSpec((tokens, LANES), functools.partial(column_map, delta, chunk, chunks))
        for delta in deltas
    ]
    taps_spec = [pl.BlockSpec(taps.shape, lambda step, seq_ref: (0, 0))] if with_taps else []
    scratch = [pltpu.VMEM((blocks, tap_rows, LANES), jnp.float32)] if with_taps else []
    made = pl.pallas_call(
        functools.partial(product_kernel, blocks, deltas, tokens, with_taps),
        out_shape=[jax.ShapeDtypeStruct((rows, LANES), jnp.bfloat16)] * count,
        grid_spec=pltpu.PrefetchScalarGridSpec(
            num_scalar_prefetch=1,
            grid=(1,),
            in_specs=column + column + taps_spec,
            out_specs=[pl.BlockSpec((rows, LANES), lambda step, seq_ref: (0, 0))] * count,
            scratch_shapes=scratch,
        ),
        cost_estimate=pl.CostEstimate(
            flops=tokens * LANES * count, bytes_accessed=6 * tokens * LANES * count, transcendentals=0
        ),
        compiler_params=pltpu.CompilerParams(vmem_limit_bytes=vmem_bytes),
    )(seq_index, *[key_gate] * count, *[value_input] * count, *([taps] if with_taps else []))
    return dict(zip(deltas, made))


def column_map(delta, chunk, chunks, step, seq_ref):
    return (0, (seq_ref[0] ^ delta) * chunks + chunk)


def fill_table(table, lines, block, per_chunk):
    def one_line(group, index):
        at = index % 4
        return lines[group, block + 1 + (index - at) // 4, pl.ds(at, 1), :]

    for group in range(per_chunk):
        for index in range(-1, 4):
            base = jnp.concatenate([one_line(group, index), one_line(group, index - 1)], axis=1)
            wide = jnp.broadcast_to(base, (LANES, 2 * LANES))
            turned = pltpu.roll(wide, 1, 1, stride=1, stride_axis=0)
            square = turned[:, LANES:].astype(jnp.bfloat16)
            for row, col, want in (
                (0, 0, 0), (1, 0, 1), (0, 1, -1), (1, 1, 0),
                (0, 2, 2), (1, 2, 3), (0, 3, 1), (1, 3, 2),
            ):
                if want == index:
                    rows = pl.ds(group * HALF + row * LANES, LANES)
                    table[rows, pl.ds(block * 2 * HALF + col * LANES, LANES)] = square


def conv_kernel(blocks, per_chunk, chunk, seq_ref, *refs):
    pieces, taps, outs = refs[:blocks], refs[blocks : 2 * blocks], refs[-blocks - 4 : -4]
    past, table, lines, results = refs[-4:]
    last = 2 * blocks - 1
    lines[...] = jnp.zeros_like(lines)
    past[pl.ds(2 * blocks * HALF, HALF), :] = jnp.zeros((HALF, LANES), jnp.bfloat16)
    for delta in range(blocks):
        source = seq_ref[0] ^ delta
        rows = taps[delta][...].astype(jnp.float32)
        groups = rows.shape[0] // 4
        for group in range(per_chunk):
            for part in range(4):
                row = part * groups + chunk * per_chunk + group
                lines[group, source + 1, pl.ds(part, 1), :] = rows[row : row + 1]
        for part in range(2):
            place = pl.multiple_of((last - part - 2 * source) * HALF, HALF)
            past[pl.ds(place, HALF), :] = pieces[delta][pl.ds(part * HALF, HALF), :]
    lane = lax.broadcasted_iota(jnp.int32, (HALF, LANES), 1) * per_chunk // LANES
    for target in range(blocks):
        fill_table(table, lines, target, per_chunk)
        depth = (target + 1) * 2 * HALF
        left = past[pl.ds((last - 2 * target) * HALF, depth), :]
        right = past[pl.ds((last - 2 * target - 1) * HALF, depth), :]
        total = jnp.dot(
            table[:, pl.ds(0, depth)],
            jnp.concatenate([left, right], axis=1),
            preferred_element_type=jnp.float32,
        )
        for part in range(2):
            columns = slice(part * LANES, (part + 1) * LANES)
            chosen = total[:HALF, columns]
            for group in range(1, per_chunk):
                chosen = jnp.where(lane == group, total[group * HALF : (group + 1) * HALF, columns], chosen)
            results[target, pl.ds(part * HALF, HALF), :] = chosen.astype(jnp.bfloat16)
    for delta in range(blocks):
        outs[delta][...] = results[seq_ref[0] ^ delta]


def make_conv(seq_index, pieces, taps, blocks, tokens, groups, chunk, chunks, after):
    per_chunk = groups // chunks
    tap_rows = taps[0].shape[0] - tokens
    flops = 4 * HALF * HALF * HALF * per_chunk * blocks * (blocks + 1)
    return pl.pallas_call(
        functools.partial(conv_kernel, blocks, per_chunk, chunk),
        out_shape=[jax.ShapeDtypeStruct((tokens, LANES), jnp.bfloat16)] * blocks,
        grid_spec=pltpu.PrefetchScalarGridSpec(
            num_scalar_prefetch=1,
            grid=(1,),
            in_specs=[pl.BlockSpec((tokens, LANES), lambda step, seq_ref: (0, 0))] * blocks
            + [pl.BlockSpec((tap_rows, LANES), lambda step, seq_ref: (tokens // tap_rows, 0))] * blocks
            + [ANYWHERE] * len(after),
            out_specs=[pl.BlockSpec((tokens, LANES), lambda step, seq_ref: (0, 0))] * blocks,
            scratch_shapes=[
                pltpu.VMEM(((2 * blocks + 1) * HALF, LANES), jnp.bfloat16),
                pltpu.VMEM((per_chunk * HALF, 2 * blocks * HALF), jnp.bfloat16),
                pltpu.VMEM((per_chunk, blocks + 1, 8, LANES), jnp.float32),
                pltpu.VMEM((blocks, tokens, LANES), jnp.bfloat16),
            ],
        ),
        cost_estimate=pl.CostEstimate(
            flops=flops, bytes_accessed=4 * blocks * tokens * LANES, transcendentals=0
        ),
        compiler_params=pltpu.CompilerParams(vmem_limit_bytes=VMEM_BYTES),
    )(seq_index, *pieces, *taps, *after)


def squares_kernel(blocks, seq_ref, *refs):
    gates, pieces, carried, out = refs[:blocks], refs[blocks : 2 * blocks], refs[2 * blocks : -1], refs[-1]
    total = None
    for delta in range(blocks):
        gated = gates[delta][...].astype(jnp.float32) * pieces[delta][...].astype(jnp.float32)
        total = gated * gated if total is None else total + gated * gated
    line = jnp.sum(jnp.transpose(total), axis=0, keepdims=True)
    for earlier in carried:
        line += earlier[...]
    out[...] = line


def make_squares(seq_index, query_gate, pieces, blocks, chunk, chunks, carried):
    tokens = query_gate.shape[0]
    return pl.pallas_call(
        functools.partial(squares_kernel, blocks),
        out_shape=jax.ShapeDtypeStruct((1, tokens), jnp.float32),
        grid_spec=pltpu.PrefetchScalarGridSpec(
            num_scalar_prefetch=1,
            grid=(1,),
            in_specs=[
                pl.BlockSpec((tokens, LANES), functools.partial(column_map, delta, chunk, chunks))
                for delta in range(blocks)
            ]
            + [pl.BlockSpec((tokens, LANES), lambda step, seq_ref: (0, 0))] * blocks
            + [pl.BlockSpec((1, tokens), lambda step, seq_ref: (0, 0))] * len(carried),
            out_specs=pl.BlockSpec((1, tokens), lambda step, seq_ref: (0, 0)),
        ),
        cost_estimate=pl.CostEstimate(
            flops=3 * tokens * LANES * blocks, bytes_accessed=4 * tokens * LANES * blocks, transcendentals=0
        ),
        compiler_params=pltpu.CompilerParams(vmem_limit_bytes=SMALL_BYTES),
    )(seq_index, *[query_gate] * blocks, *pieces, *carried)


def gate_kernel(blocks, chunk, chunks, seq_ref, *refs):
    gates, pieces = refs[:blocks], refs[blocks : 2 * blocks]
    out_ref, staged, sems = refs[-3:]
    copies = []
    for delta in range(blocks):
        gated = gates[delta][...].astype(jnp.float32) * pieces[delta][...].astype(jnp.float32)
        staged[delta] = gated.astype(jnp.bfloat16)
        place = pl.multiple_of(((seq_ref[0] ^ delta) * chunks + chunk) * LANES, LANES)
        copies.append(
            pltpu.make_async_copy(staged.at[delta], out_ref.at[:, pl.ds(place, LANES)], sems.at[delta])
        )
        copies[-1].start()
    for copy in copies:
        copy.wait()


def make_gate(seq_index, query_gate, pieces, blocks, chunk, chunks, so_far):
    tokens, channels = query_gate.shape
    return pl.pallas_call(
        functools.partial(gate_kernel, blocks, chunk, chunks),
        out_shape=jax.ShapeDtypeStruct((tokens, channels), jnp.bfloat16),
        grid_spec=pltpu.PrefetchScalarGridSpec(
            num_scalar_prefetch=1,
            grid=(1,),
            in_specs=[
                pl.BlockSpec((tokens, LANES), functools.partial(column_map, delta, chunk, chunks))
                for delta in range(blocks)
            ]
            + [pl.BlockSpec((tokens, LANES), lambda step, seq_ref: (0, 0))] * blocks
            + [ANYWHERE] * len(so_far),
            out_specs=ANYWHERE,
            scratch_shapes=[
                pltpu.VMEM((blocks, tokens, LANES), jnp.bfloat16),
                pltpu.SemaphoreType.DMA((blocks,)),
            ],
        ),
        input_output_aliases={2 * blocks + 1: 0} if so_far else {},
        cost_estimate=pl.CostEstimate(
            flops=tokens * LANES * blocks, bytes_accessed=6 * tokens * LANES * blocks, transcendentals=0
        ),
        compiler_params=pltpu.CompilerParams(vmem_limit_bytes=SMALL_BYTES),
    )(seq_index, *[query_gate] * blocks, *pieces, *so_far)


def finish_kernel(blocks, chunks, parts, seq_ref, gate_ref, gain_ref, *refs):
    sums, pieces, normed_ref = refs[:parts], refs[parts:-1], refs[-1]
    rows = gate_ref.shape[0]
    square_sum = sums[0][...]
    for part in sums[1:]:
        square_sum = square_sum + part[...]
    inverse = lax.rsqrt(square_sum / D + norm_eps)
    scale = jnp.transpose(jnp.broadcast_to(inverse, (LANES, rows)))
    for delta in range(blocks):
        for chunk in range(chunks):
            place = pl.multiple_of(((seq_ref[0] ^ delta) * chunks + chunk) * LANES, LANES)
            columns = pl.ds(place, LANES)
            piece = pieces[chunk * blocks + delta][...].astype(jnp.float32)
            gated = gate_ref[:, columns].astype(jnp.float32) * piece
            normed_ref[:, columns] = (gated * scale * gain_ref[:, columns]).astype(jnp.bfloat16)


def make_finish(seq_index, query_gate, norm_gain, sums, pieces, blocks, chunks):
    tokens, channels = query_gate.shape
    rows = FINISH_ROWS
    row_spec = pl.BlockSpec((rows, channels), lambda step, seq_ref: (step, 0))
    return pl.pallas_call(
        functools.partial(finish_kernel, blocks, chunks, len(sums)),
        out_shape=jax.ShapeDtypeStruct((tokens, channels), jnp.bfloat16),
        grid_spec=pltpu.PrefetchScalarGridSpec(
            num_scalar_prefetch=1,
            grid=(tokens // rows,),
            in_specs=[
                row_spec,
                pl.BlockSpec((1, channels), lambda step, seq_ref: (0, 0)),
            ]
            + [pl.BlockSpec((1, rows), lambda step, seq_ref: (0, step))] * len(sums)
            + [pl.BlockSpec((rows, LANES), lambda step, seq_ref: (step, 0))] * (blocks * chunks),
            out_specs=row_spec,
        ),
        cost_estimate=pl.CostEstimate(
            flops=4 * tokens * channels, bytes_accessed=8 * tokens * channels, transcendentals=tokens
        ),
        compiler_params=pltpu.CompilerParams(vmem_limit_bytes=SMALL_BYTES),
        name="finish",
    )(seq_index, query_gate, norm_gain[None, :], *sums, *pieces)


def exchange(pieces, blocks, turn):
    moved = {}
    for delta in ORDERS[turn]:
        moved[delta] = lax.ppermute(pieces[delta], "seq", pairs_of(blocks, delta))
    return [pieces[0]] + [moved[delta] for delta in range(1, blocks)]


def tiles_fit(tokens, channels, groups, blocks, width):
    if width & (width - 1) or blocks & (blocks - 1) or tokens != 2 * HALF or channels % (blocks * LANES):
        return False
    width_here, group_width = channels // blocks, channels // groups
    return LANES % group_width == 0 and width_here % group_width == 0


def body(query_gate, key_gate, value_input, filter_taps, norm_gain):
    tokens, channels = key_gate.shape
    blocks = lax.axis_size("seq")
    groups_here = filter_taps.shape[1]
    if not tiles_fit(tokens, channels, groups_here, blocks, lax.axis_size("chan")):
        return dense_body(query_gate, key_gate, value_input, filter_taps, norm_gain)
    chunks = channels // (blocks * LANES)
    groups = groups_here // blocks
    seq_index = lax.axis_index("seq").astype(jnp.int32)[None]
    taps = jnp.transpose(filter_taps)

    return tiled_body(
        seq_index, query_gate, key_gate, value_input, taps, norm_gain, blocks, groups, chunks
    )


def tiled_body(seq_index, query_gate, key_gate, value_input, taps, norm_gain, blocks, groups, chunks):
    tokens = key_gate.shape[0]
    received = []
    for chunk in range(chunks):
        sent = {}
        splits = (range(blocks // 2, blocks), range(blocks // 2)) if chunk == 0 else (range(blocks),)
        for turn, deltas in enumerate(splits):
            made = make_product(
                seq_index, key_gate, value_input, None if chunk else taps,
                blocks, tuple(deltas), chunk, chunks,
                FIRST_BYTES if chunk == 0 and turn == 0 else PRODUCT_BYTES,
            )
            sent.update(made)
        received.append(exchange(sent, blocks, chunk))
    returned = []
    after = []
    for chunk in range(chunks):
        local = make_conv(seq_index, received[chunk], received[0], blocks, tokens, groups, chunk, chunks, after)
        after = local[:1]
        returned.append(exchange(local, blocks, chunks + chunk))
    square_sum, gated = [], []
    for chunk in range(chunks):
        square_sum = [make_squares(seq_index, query_gate, returned[chunk], blocks, chunk, chunks, square_sum)]
        gated = [make_gate(seq_index, query_gate, returned[chunk], blocks, chunk, chunks, gated)]
    width = lax.axis_size("chan")
    sums = list(square_sum)
    for delta in range(width - 1, 0, -1):
        sums.append(lax.ppermute(square_sum[0], "chan", pairs_of(width, delta)))
    pieces = [piece for chunk in returned for piece in chunk]
    normed = make_finish(
        seq_index, query_gate, norm_gain, sums, pieces, blocks, chunks
    )
    return (gated[0], normed)


def solution(mesh):
    placed = (P("seq", "chan"), P("seq", "chan"), P("seq", "chan"), P("seq", "chan"), P("chan"))
    return jax.shard_map(
        body,
        mesh=mesh,
        in_specs=placed,
        out_specs=(P("seq", "chan"), P("seq", "chan")),
        check_vma=False,
    )
```

```python
import functools
import math

import jax
import jax.numpy as jnp
from jax import lax
from jax.experimental import pallas as pl
from jax.experimental.pallas import tpu as pltpu
from jax.sharding import PartitionSpec as P


D = 8192
GROUPS = 128


norm_eps = 1e-05


def angle_table(rows_count, cols_count, period):
    row_ids = lax.iota(jnp.int32, rows_count)
    col_ids = lax.iota(jnp.int32, cols_count)
    phases = row_ids[:, None] * col_ids[None, :] % period
    return phases.astype(jnp.float32) * (2.0 * math.pi / period)


def block_matrix(rows_count, cols_count, period):
    phases = angle_table(rows_count, cols_count, period)
    return jnp.stack([jnp.cos(phases), -jnp.sin(phases)]).astype(jnp.bfloat16)


def line_matrix(length, direction):
    phases = angle_table(length, length, length)
    cosine = jnp.cos(phases)
    sine_part = jnp.sin(phases) * direction
    upper = jnp.concatenate([cosine, sine_part], axis=1)
    lower = jnp.concatenate([-sine_part, cosine], axis=1)
    return jnp.concatenate([upper, lower], axis=0).astype(jnp.bfloat16)


def twiddle_minor(real_in, imag_in, period, direction):
    phases = angle_table(real_in.shape[1], real_in.shape[2], period)
    cosine = jnp.cos(phases)[None, :, :]
    sine_part = direction * jnp.sin(phases)[None, :, :]
    real_part = real_in * cosine - imag_in * sine_part
    imaginary = imag_in * cosine + real_in * sine_part
    return (real_part, imaginary)


def spectrum_minor(rows_in, first_matrix, right_forward, periods):
    spread = jnp.einsum("cab,rak->rckb", rows_in, first_matrix, preferred_element_type=jnp.float32)
    real_part, imaginary = twiddle_minor(spread[0], spread[1], periods, -1.0)
    joined = jnp.concatenate(
        [real_part.astype(jnp.bfloat16), imaginary.astype(jnp.bfloat16)], axis=2
    )
    return jnp.einsum("ckb,bm->ckm", joined, right_forward, preferred_element_type=jnp.float32)


def dense_body(query_gate, key_gate, value_input, filter_taps, norm_gain):
    tokens, channels = key_gate.shape
    blocks = lax.axis_size("seq")
    periods = 2 * tokens * blocks
    product = (key_gate.astype(jnp.float32) * value_input.astype(jnp.float32)).astype(jnp.bfloat16)
    first_matrix = block_matrix(blocks, 2 * blocks, 2 * blocks)
    last_matrix = block_matrix(2 * blocks, blocks, 2 * blocks)
    line_forward = line_matrix(tokens, 1.0)
    line_backward = line_matrix(tokens, -1.0)
    width_here = channels // blocks
    group_width = D // GROUPS
    repeat_count = max(1, group_width // width_here)
    taps_wide = jnp.repeat(filter_taps, repeat_count, axis=1)
    data_major = jnp.transpose(product)
    taps_major = jnp.transpose(taps_wide)
    data_whole, taps_whole = (
        lax.all_to_all(data_major, "seq", split_axis=0, concat_axis=1, tiled=True),
        lax.all_to_all(taps_major, "seq", split_axis=0, concat_axis=1, tiled=True),
    )
    taps_cols = taps_whole.shape[0]
    data_rows = data_whole.reshape(width_here, blocks, tokens)
    taps_rows = taps_whole.reshape(taps_cols, blocks, tokens)
    right_forward = jnp.transpose(line_forward)
    right_backward = jnp.transpose(line_backward)
    spectrum = spectrum_minor(data_rows, first_matrix, right_forward, periods)
    taps_spectrum = spectrum_minor(taps_rows, first_matrix, right_forward, periods)
    grouped = spectrum.reshape(taps_cols, width_here // taps_cols, 2 * blocks, 2 * tokens)
    spec_real = grouped[..., :tokens]
    spec_imag = grouped[..., tokens:]
    filter_real = taps_spectrum[:, None, :, :tokens]
    filter_imag = taps_spectrum[:, None, :, tokens:]
    filtered_real = (spec_real * filter_real - spec_imag * filter_imag).astype(jnp.bfloat16)
    filtered_imag = (spec_real * filter_imag + spec_imag * filter_real).astype(jnp.bfloat16)
    filtered = jnp.concatenate([filtered_real, filtered_imag], axis=3).reshape(
        width_here, 2 * blocks, 2 * tokens
    )
    inverted = jnp.einsum(
        "ckm,mb->ckb", filtered, right_backward, preferred_element_type=jnp.float32
    )
    back_real, back_imag = twiddle_minor(
        inverted[..., :tokens], inverted[..., tokens:], periods, 1.0
    )
    returned = jnp.stack([back_real, back_imag]).astype(jnp.bfloat16)
    summed = jnp.einsum("rckb,rka->cab", returned, last_matrix, preferred_element_type=jnp.float32)
    local_blocks = (
        (summed * (1.0 / periods)).astype(jnp.bfloat16).reshape(width_here, blocks * tokens)
    )
    convolved_major = lax.all_to_all(local_blocks, "seq", split_axis=1, concat_axis=0, tiled=True)
    convolved = jnp.transpose(convolved_major)
    gated_full = query_gate.astype(jnp.float32) * convolved.astype(jnp.float32)
    partial_squares = jnp.sum(gated_full * gated_full, axis=1)
    square_sum = lax.psum(partial_squares, "chan")
    inverse_rms = lax.rsqrt(square_sum / D + norm_eps)
    normed = gated_full * inverse_rms[:, None] * norm_gain[None, :]
    return (gated_full.astype(jnp.bfloat16), normed.astype(jnp.bfloat16))


LANES = 128
HALF = 256
VMEM_BYTES = 20 << 20
SMALL_BYTES = 14 << 20
FIRST_BYTES = 62 << 20
PRODUCT_BYTES = 58 << 20
ANYWHERE = pl.BlockSpec(memory_space=pl.ANY)
ORDERS = (
    (6, 7, 4, 5, 2, 3, 1),
    (1, 2, 3, 4, 5, 6, 7),
    (1, 2, 3, 4, 5, 6, 7),
    (1, 2, 3, 4, 5, 6, 7),
)
FINISH_ROWS = 128


def pairs_of(blocks, delta):
    return [(source, source ^ delta) for source in range(blocks)]


def tap_rows_of(taps_ref, rows_ref, blocks):
    groups, count = taps_ref.shape[0] // blocks, taps_ref.shape[1] // LANES
    mirror = lax.broadcasted_iota(jnp.int32, (LANES, LANES), 0) + lax.broadcasted_iota(
        jnp.int32, (LANES, LANES), 1
    )
    mirror = (mirror == LANES - 1).astype(jnp.float32).astype(jnp.bfloat16)
    for part in range(count):
        line = taps_ref[:, pl.ds(part * LANES, LANES)]
        line = jnp.dot(line, mirror, preferred_element_type=jnp.float32)
        for block in range(blocks):
            rows_ref[block, pl.ds(part * groups, groups), :] = line[block * groups : (block + 1) * groups]


def product_kernel(blocks, deltas, tokens, with_taps, seq_ref, *refs):
    count = len(deltas)
    keys, values = refs[:count], refs[count : 2 * count]
    outs = refs[-count - 1 : -1] if with_taps else refs[-count:]
    if with_taps:
        taps_ref, rows_ref = refs[2 * count], refs[-1]
        tap_rows_of(taps_ref, rows_ref, blocks)
    for index, delta in enumerate(deltas):
        wide = keys[index][...].astype(jnp.float32) * values[index][...].astype(jnp.float32)
        outs[index][pl.ds(0, tokens), :] = wide.astype(jnp.bfloat16)
        if with_taps:
            lines = rows_ref[seq_ref[0] ^ delta]
            outs[index][pl.ds(tokens, lines.shape[0]), :] = lines.astype(jnp.bfloat16)


def make_product(seq_index, key_gate, value_input, taps, blocks, deltas, chunk, chunks, vmem_bytes):
    tokens, count = key_gate.shape[0], len(deltas)
    with_taps = taps is not None
    tap_rows = taps.size // (blocks * LANES) if with_taps else 0
    rows = tokens + tap_rows
    column = [
        pl.BlockSpec((tokens, LANES), functools.partial(column_map, delta, chunk, chunks))
        for delta in deltas
    ]
    taps_spec = [pl.BlockSpec(taps.shape, lambda step, seq_ref: (0, 0))] if with_taps else []
    scratch = [pltpu.VMEM((blocks, tap_rows, LANES), jnp.float32)] if with_taps else []
    made = pl.pallas_call(
        functools.partial(product_kernel, blocks, deltas, tokens, with_taps),
        out_shape=[jax.ShapeDtypeStruct((rows, LANES), jnp.bfloat16)] * count,
        grid_spec=pltpu.PrefetchScalarGridSpec(
            num_scalar_prefetch=1,
            grid=(1,),
            in_specs=column + column + taps_spec,
            out_specs=[pl.BlockSpec((rows, LANES), lambda step, seq_ref: (0, 0))] * count,
            scratch_shapes=scratch,
        ),
        cost_estimate=pl.CostEstimate(
            flops=tokens * LANES * count, bytes_accessed=6 * tokens * LANES * count, transcendentals=0
        ),
        compiler_params=pltpu.CompilerParams(vmem_limit_bytes=vmem_bytes),
    )(seq_index, *[key_gate] * count, *[value_input] * count, *([taps] if with_taps else []))
    return dict(zip(deltas, made))


def column_map(delta, chunk, chunks, step, seq_ref):
    return (0, (seq_ref[0] ^ delta) * chunks + chunk)


def fill_table(table, lines, block, per_chunk):
    def one_line(group, index):
        at = index % 4
        return lines[group, block + 1 + (index - at) // 4, pl.ds(at, 1), :]

    for group in range(per_chunk):
        for index in range(-1, 4):
            base = jnp.concatenate([one_line(group, index), one_line(group, index - 1)], axis=1)
            wide = jnp.broadcast_to(base, (LANES, 2 * LANES))
            turned = pltpu.roll(wide, 1, 1, stride=1, stride_axis=0)
            square = turned[:, LANES:].astype(jnp.bfloat16)
            for row, col, want in (
                (0, 0, 0), (1, 0, 1), (0, 1, -1), (1, 1, 0),
                (0, 2, 2), (1, 2, 3), (0, 3, 1), (1, 3, 2),
            ):
                if want == index:
                    rows = pl.ds(group * HALF + row * LANES, LANES)
                    table[rows, pl.ds(block * 2 * HALF + col * LANES, LANES)] = square


def conv_kernel(blocks, per_chunk, chunk, seq_ref, *refs):
    pieces, taps, outs = refs[:blocks], refs[blocks : 2 * blocks], refs[-blocks - 4 : -4]
    past, table, lines, results = refs[-4:]
    last = 2 * blocks - 1
    lines[...] = jnp.zeros_like(lines)
    past[pl.ds(2 * blocks * HALF, HALF), :] = jnp.zeros((HALF, LANES), jnp.bfloat16)
    for delta in range(blocks):
        source = seq_ref[0] ^ delta
        rows = taps[delta][...].astype(jnp.float32)
        groups = rows.shape[0] // 4
        for group in range(per_chunk):
            for part in range(4):
                row = part * groups + chunk * per_chunk + group
                lines[group, source + 1, pl.ds(part, 1), :] = rows[row : row + 1]
        for part in range(2):
            place = pl.multiple_of((last - part - 2 * source) * HALF, HALF)
            past[pl.ds(place, HALF), :] = pieces[delta][pl.ds(part * HALF, HALF), :]
    lane = lax.broadcasted_iota(jnp.int32, (HALF, LANES), 1) * per_chunk // LANES
    for target in range(blocks):
        fill_table(table, lines, target, per_chunk)
        depth = (target + 1) * 2 * HALF
        left = past[pl.ds((last - 2 * target) * HALF, depth), :]
        right = past[pl.ds((last - 2 * target - 1) * HALF, depth), :]
        total = jnp.dot(
            table[:, pl.ds(0, depth)],
            jnp.concatenate([left, right], axis=1),
            preferred_element_type=jnp.float32,
        )
        for part in range(2):
            columns = slice(part * LANES, (part + 1) * LANES)
            chosen = total[:HALF, columns]
            for group in range(1, per_chunk):
                chosen = jnp.where(lane == group, total[group * HALF : (group + 1) * HALF, columns], chosen)
            results[target, pl.ds(part * HALF, HALF), :] = chosen.astype(jnp.bfloat16)
    for delta in range(blocks):
        outs[delta][...] = results[seq_ref[0] ^ delta]


def make_conv(seq_index, pieces, taps, blocks, tokens, groups, chunk, chunks, after):
    per_chunk = groups // chunks
    tap_rows = taps[0].shape[0] - tokens
    flops = 4 * HALF * HALF * HALF * per_chunk * blocks * (blocks + 1)
    return pl.pallas_call(
        functools.partial(conv_kernel, blocks, per_chunk, chunk),
        out_shape=[jax.ShapeDtypeStruct((tokens, LANES), jnp.bfloat16)] * blocks,
        grid_spec=pltpu.PrefetchScalarGridSpec(
            num_scalar_prefetch=1,
            grid=(1,),
            in_specs=[pl.BlockSpec((tokens, LANES), lambda step, seq_ref: (0, 0))] * blocks
            + [pl.BlockSpec((tap_rows, LANES), lambda step, seq_ref: (tokens // tap_rows, 0))] * blocks
            + [ANYWHERE] * len(after),
            out_specs=[pl.BlockSpec((tokens, LANES), lambda step, seq_ref: (0, 0))] * blocks,
            scratch_shapes=[
                pltpu.VMEM(((2 * blocks + 1) * HALF, LANES), jnp.bfloat16),
                pltpu.VMEM((per_chunk * HALF, 2 * blocks * HALF), jnp.bfloat16),
                pltpu.VMEM((per_chunk, blocks + 1, 8, LANES), jnp.float32),
                pltpu.VMEM((blocks, tokens, LANES), jnp.bfloat16),
            ],
        ),
        cost_estimate=pl.CostEstimate(
            flops=flops, bytes_accessed=4 * blocks * tokens * LANES, transcendentals=0
        ),
        compiler_params=pltpu.CompilerParams(vmem_limit_bytes=VMEM_BYTES),
    )(seq_index, *pieces, *taps, *after)


def squares_kernel(blocks, seq_ref, *refs):
    gates, pieces, carried, out = refs[:blocks], refs[blocks : 2 * blocks], refs[2 * blocks : -1], refs[-1]
    total = None
    for delta in range(blocks):
        gated = gates[delta][...].astype(jnp.float32) * pieces[delta][...].astype(jnp.float32)
        total = gated * gated if total is None else total + gated * gated
    line = jnp.sum(jnp.transpose(total), axis=0, keepdims=True)
    for earlier in carried:
        line += earlier[...]
    out[...] = line


def make_squares(seq_index, query_gate, pieces, blocks, chunk, chunks, carried):
    tokens = query_gate.shape[0]
    return pl.pallas_call(
        functools.partial(squares_kernel, blocks),
        out_shape=jax.ShapeDtypeStruct((1, tokens), jnp.float32),
        grid_spec=pltpu.PrefetchScalarGridSpec(
            num_scalar_prefetch=1,
            grid=(1,),
            in_specs=[
                pl.BlockSpec((tokens, LANES), functools.partial(column_map, delta, chunk, chunks))
                for delta in range(blocks)
            ]
            + [pl.BlockSpec((tokens, LANES), lambda step, seq_ref: (0, 0))] * blocks
            + [pl.BlockSpec((1, tokens), lambda step, seq_ref: (0, 0))] * len(carried),
            out_specs=pl.BlockSpec((1, tokens), lambda step, seq_ref: (0, 0)),
        ),
        cost_estimate=pl.CostEstimate(
            flops=3 * tokens * LANES * blocks, bytes_accessed=4 * tokens * LANES * blocks, transcendentals=0
        ),
        compiler_params=pltpu.CompilerParams(vmem_limit_bytes=SMALL_BYTES),
    )(seq_index, *[query_gate] * blocks, *pieces, *carried)


def gate_kernel(blocks, chunk, chunks, seq_ref, *refs):
    gates, pieces = refs[:blocks], refs[blocks : 2 * blocks]
    out_ref, staged, sems = refs[-3:]
    copies = []
    for delta in range(blocks):
        gated = gates[delta][...].astype(jnp.float32) * pieces[delta][...].astype(jnp.float32)
        staged[delta] = gated.astype(jnp.bfloat16)
        place = pl.multiple_of(((seq_ref[0] ^ delta) * chunks + chunk) * LANES, LANES)
        copies.append(
            pltpu.make_async_copy(staged.at[delta], out_ref.at[:, pl.ds(place, LANES)], sems.at[delta])
        )
        copies[-1].start()
    for copy in copies:
        copy.wait()


def make_gate(seq_index, query_gate, pieces, blocks, chunk, chunks, so_far):
    tokens, channels = query_gate.shape
    return pl.pallas_call(
        functools.partial(gate_kernel, blocks, chunk, chunks),
        out_shape=jax.ShapeDtypeStruct((tokens, channels), jnp.bfloat16),
        grid_spec=pltpu.PrefetchScalarGridSpec(
            num_scalar_prefetch=1,
            grid=(1,),
            in_specs=[
                pl.BlockSpec((tokens, LANES), functools.partial(column_map, delta, chunk, chunks))
                for delta in range(blocks)
            ]
            + [pl.BlockSpec((tokens, LANES), lambda step, seq_ref: (0, 0))] * blocks
            + [ANYWHERE] * len(so_far),
            out_specs=ANYWHERE,
            scratch_shapes=[
                pltpu.VMEM((blocks, tokens, LANES), jnp.bfloat16),
                pltpu.SemaphoreType.DMA((blocks,)),
            ],
        ),
        input_output_aliases={2 * blocks + 1: 0} if so_far else {},
        cost_estimate=pl.CostEstimate(
            flops=tokens * LANES * blocks, bytes_accessed=6 * tokens * LANES * blocks, transcendentals=0
        ),
        compiler_params=pltpu.CompilerParams(vmem_limit_bytes=SMALL_BYTES),
    )(seq_index, *[query_gate] * blocks, *pieces, *so_far)


def finish_kernel(blocks, chunks, parts, seq_ref, gate_ref, gain_ref, *refs):
    sums, pieces = refs[:parts], refs[parts:-3]
    normed_ref, staged, sems = refs[-3:]
    rows = FINISH_ROWS
    copies = []
    for turn in range(gate_ref.shape[0] // rows):
        lines = pl.ds(turn * rows, rows)
        square_sum = sums[0][:, lines]
        for part in sums[1:]:
            square_sum = square_sum + part[:, lines]
        inverse = lax.rsqrt(square_sum / D + norm_eps)
        scale = jnp.transpose(jnp.broadcast_to(inverse, (LANES, rows)))
        for delta in range(blocks):
            for chunk in range(chunks):
                place = pl.multiple_of(((seq_ref[0] ^ delta) * chunks + chunk) * LANES, LANES)
                columns = pl.ds(place, LANES)
                piece = pieces[chunk * blocks + delta][lines, :].astype(jnp.float32)
                gated = gate_ref[lines, columns].astype(jnp.float32) * piece
                staged[lines, columns] = (gated * scale * gain_ref[:, columns]).astype(jnp.bfloat16)
        copies.append(
            pltpu.make_async_copy(staged.at[lines, :], normed_ref.at[lines, :], sems.at[turn])
        )
        copies[-1].start()
    for copy in copies:
        copy.wait()


def make_finish(seq_index, query_gate, norm_gain, sums, pieces, blocks, chunks):
    tokens, channels = query_gate.shape
    return pl.pallas_call(
        functools.partial(finish_kernel, blocks, chunks, len(sums)),
        out_shape=jax.ShapeDtypeStruct((tokens, channels), jnp.bfloat16),
        grid_spec=pltpu.PrefetchScalarGridSpec(
            num_scalar_prefetch=1,
            grid=(1,),
            in_specs=[
                pl.BlockSpec((tokens, channels), lambda step, seq_ref: (0, 0)),
                pl.BlockSpec((1, channels), lambda step, seq_ref: (0, 0)),
            ]
            + [pl.BlockSpec((1, tokens), lambda step, seq_ref: (0, 0))] * len(sums)
            + [pl.BlockSpec((tokens, LANES), lambda step, seq_ref: (0, 0))] * (blocks * chunks),
            out_specs=ANYWHERE,
            scratch_shapes=[
                pltpu.VMEM((tokens, channels), jnp.bfloat16),
                pltpu.SemaphoreType.DMA((tokens // FINISH_ROWS,)),
            ],
        ),
        cost_estimate=pl.CostEstimate(
            flops=4 * tokens * channels, bytes_accessed=6 * tokens * channels, transcendentals=tokens
        ),
        compiler_params=pltpu.CompilerParams(vmem_limit_bytes=SMALL_BYTES),
        name="finish",
    )(seq_index, query_gate, norm_gain[None, :], *sums, *pieces)


def exchange(pieces, blocks, turn):
    moved = {}
    for delta in ORDERS[turn]:
        moved[delta] = lax.ppermute(pieces[delta], "seq", pairs_of(blocks, delta))
    return [pieces[0]] + [moved[delta] for delta in range(1, blocks)]


def tiles_fit(tokens, channels, groups, blocks, width):
    if width & (width - 1) or blocks & (blocks - 1) or tokens != 2 * HALF or channels % (blocks * LANES):
        return False
    width_here, group_width = channels // blocks, channels // groups
    return LANES % group_width == 0 and width_here % group_width == 0


def body(query_gate, key_gate, value_input, filter_taps, norm_gain):
    tokens, channels = key_gate.shape
    blocks = lax.axis_size("seq")
    groups_here = filter_taps.shape[1]
    if not tiles_fit(tokens, channels, groups_here, blocks, lax.axis_size("chan")):
        return dense_body(query_gate, key_gate, value_input, filter_taps, norm_gain)
    chunks = channels // (blocks * LANES)
    groups = groups_here // blocks
    seq_index = lax.axis_index("seq").astype(jnp.int32)[None]
    taps = jnp.transpose(filter_taps)

    return tiled_body(
        seq_index, query_gate, key_gate, value_input, taps, norm_gain, blocks, groups, chunks
    )


def tiled_body(seq_index, query_gate, key_gate, value_input, taps, norm_gain, blocks, groups, chunks):
    tokens = key_gate.shape[0]
    received = []
    for chunk in range(chunks):
        sent = {}
        splits = (range(blocks // 2, blocks), range(blocks // 2)) if chunk == 0 else (range(blocks),)
        for turn, deltas in enumerate(splits):
            made = make_product(
                seq_index, key_gate, value_input, None if chunk else taps,
                blocks, tuple(deltas), chunk, chunks,
                FIRST_BYTES if chunk == 0 and turn == 0 else PRODUCT_BYTES,
            )
            sent.update(made)
        received.append(exchange(sent, blocks, chunk))
    returned = []
    after = []
    for chunk in range(chunks):
        local = make_conv(seq_index, received[chunk], received[0], blocks, tokens, groups, chunk, chunks, after)
        after = local[:1]
        returned.append(exchange(local, blocks, chunks + chunk))
    square_sum, gated = [], []
    for chunk in range(chunks):
        square_sum = [make_squares(seq_index, query_gate, returned[chunk], blocks, chunk, chunks, square_sum)]
        gated = [make_gate(seq_index, query_gate, returned[chunk], blocks, chunk, chunks, gated)]
    width = lax.axis_size("chan")
    sums = list(square_sum)
    for delta in range(width - 1, 0, -1):
        sums.append(lax.ppermute(square_sum[0], "chan", pairs_of(width, delta)))
    pieces = [piece for chunk in returned for piece in chunk]
    normed = make_finish(
        seq_index, query_gate, norm_gain, sums, pieces, blocks, chunks
    )
    return (gated[0], normed)


def solution(mesh):
    placed = (P("seq", "chan"), P("seq", "chan"), P("seq", "chan"), P("seq", "chan"), P("chan"))
    return jax.shard_map(
        body,
        mesh=mesh,
        in_specs=placed,
        out_specs=(P("seq", "chan"), P("seq", "chan")),
        check_vma=False,
    )
```
